32 devices in a mesh: ray: 4 (over y, core), cuts: 8 (over z, x).
Axes of the slice: x: 2, y: 2, z: 4, core: 2. Of those that a mesh axis runs over, the one named last changes fastest.
Arguments:
- initial: float32 [16, 16, 4096], P('cuts', 'ray'), may hold values from 0.5 to 1.5
- measured: float32 [4, 32, 16, 4096], P('ray', None, 'cuts'), may hold values from 9.6 to 28.8
- order: int32 [4], replicated, may hold values from 0 to 3, each once
- angle_index: int32 [4, 32], replicated, may hold values from 0 to 2999
Outputs:
- reconstruction: float32 [16, 16, 4096], P('cuts', 'ray')
The draws below stay inside these ranges and needn't reach their ends.
Inputs may be any that keep to these rules, and one draw needn't show every extreme that they name: Each stored subset appears once; the first 2 entries are the subsets run, in order, and stored subset j is held by index j of ray.
All inputs are finite; a program needn't handle non-finite values.
Results may differ from the reference program's by a relative error of at most 0.0003.
Values sent between devices are 32-bit elements; how exact they have to be, the bound alone decides.
No kernel may reach another device: no remote copies, remote signals or barrier semaphores. Data moves between devices by JAX's collectives and lax.ppermute only.
A program may use at most 64 MiB of HBM per device.

```python
import jax
import jax.numpy as jnp
from jax import lax

W = 4096
ANG = 32
SUBSETS = 2
NANG = 3000
TV_ITERS = 2
NR = 16
SLICES = 16
STORED = 4


def set_ends(result, stream_key, least, high):
    longest = result.shape.index(max(result.shape))
    spots = []
    for shift in (0, 1):
        where = [jax.random.randint(jax.random.fold_in(stream_key, axis), (), 0, length) for axis, length in enumerate(result.shape)]
        where[longest] = (where[longest] + shift) % result.shape[longest]
        spots.append(tuple(where))
    return result.at[spots[0]].set(least).at[spots[1]].set(high)


def block_scale(own_key, dims, cuts, least, high):
    factor_of, own = 1.0, jax.random.fold_in(own_key, 6)
    for axis_at, shards_of in cuts:
        heights = jnp.exp(jax.random.uniform(jax.random.fold_in(own, axis_at), (shards_of,), jnp.float32, least / len(cuts), high / len(cuts)))
        factor_of = factor_of * jnp.repeat(heights, dims[axis_at] // shards_of).reshape([-1 if axis == axis_at else 1 for axis in range(len(dims))])
    return factor_of


def setup_inputs(seed: int = 0) -> dict:
    seeds = jax.random.split(jax.random.key(seed), 5)
    return {
        "initial": jnp.clip(0.5 + 1.0 * jax.random.uniform(seeds[0], (SLICES, NR, W), jnp.float32) ** block_scale(seeds[0], (SLICES, NR, W), ((0, 8), (1, 4)), -0.2, 0.2), 0.5, 1.5),
        "measured": jnp.clip(9.6 + 19.199999 * jax.random.uniform(seeds[1], (STORED, ANG, SLICES, W), jnp.float32) ** block_scale(seeds[1], (STORED, ANG, SLICES, W), ((0, 4), (2, 8)), -0.2, 0.2), 9.6, 28.8),
        "order": jax.random.permutation(seeds[2], STORED).astype(jnp.int32),
        "angle_index": set_ends(jax.random.randint(seeds[3], (STORED, ANG), 0, NANG), jax.random.fold_in(seeds[3], 1), 0, NANG - 1).astype(jnp.int32),
    }


TV_STEP = 0.05
TV_EPS = 0.5

def geometry(angle_row):
    slopes = -1.0 + (2.0 * angle_row.astype(jnp.float32) + 1.0) / NANG
    row_pos = jnp.arange(NR, dtype=jnp.int32).astype(jnp.float32) - (NR - 1) / 2.0
    spread = slopes[:, None] * row_pos[None, :]
    floor_part = jnp.floor(spread)
    return (floor_part.astype(jnp.int32), spread - floor_part)

def project(current, shifts, fraction):
    margin = NR // 2 + 2
    padded = jnp.pad(current, ((0, 0), (0, 0), (margin, margin)))
    columns = jnp.arange(W, dtype=jnp.int32)

    def one_angle(pieces):
        shift_row, frac_row = pieces
        lead_index = columns[None, :] - shift_row[:, None] + margin
        lead_index = jnp.broadcast_to(lead_index[None], current.shape)
        near_tap = jnp.take_along_axis(padded, lead_index, axis=2)
        far_tap = jnp.take_along_axis(padded, lead_index - 1, axis=2)
        weight = frac_row[None, :, None]
        return lax.optimization_barrier(jnp.sum((1.0 - weight) * near_tap + weight * far_tap, axis=1))
    return lax.map(one_angle, (shifts, fraction))

def back_project(residual, shifts, fraction, shape):
    margin = NR // 2 + 2
    padded = jnp.pad(residual, ((0, 0), (0, 0), (margin, margin)))
    columns = jnp.arange(W, dtype=jnp.int32)

    def add_angle(summed, pieces):
        sino_plane, shift_row, frac_row = pieces
        lead_index = columns[None, :] + shift_row[:, None] + margin
        near_tap = jnp.take(sino_plane, lead_index, axis=1)
        far_tap = jnp.take(sino_plane, lead_index + 1, axis=1)
        weight = frac_row[None, :, None]
        return (summed + (1.0 - weight) * near_tap + weight * far_tap, None)
    summed, _ = lax.scan(add_angle, jnp.zeros(shape, jnp.float32), (padded, shifts, fraction))
    return summed

def tv_step(current):
    step_s = jnp.concatenate([current[1:] - current[:-1], jnp.zeros_like(current[:1])], axis=0)
    step_r = jnp.concatenate([current[:, 1:] - current[:, :-1], jnp.zeros_like(current[:, :1])], axis=1)
    step_c = jnp.concatenate([current[:, :, 1:] - current[:, :, :-1], jnp.zeros_like(current[:, :, :1])], axis=2)
    magnitude = jnp.sqrt(step_s * step_s + step_r * step_r + step_c * step_c + TV_EPS * TV_EPS)
    flow_s = step_s / magnitude
    flow_r = step_r / magnitude
    flow_c = step_c / magnitude
    spread = flow_s - jnp.concatenate([jnp.zeros_like(flow_s[:1]), flow_s[:-1]], axis=0)
    spread = spread + flow_r - jnp.concatenate([jnp.zeros_like(flow_r[:, :1]), flow_r[:, :-1]], axis=1)
    spread = spread + flow_c - jnp.concatenate([jnp.zeros_like(flow_c[:, :, :1]), flow_c[:, :, :-1]], axis=2)
    return current + TV_STEP * spread

def reference(initial, measured, order, angle_index):
    current = initial
    for subset in range(SUBSETS):
        subset_slot = order[subset]
        shifts, fraction = geometry(angle_index[subset_slot])
        forward = project(current, shifts, fraction)
        residual = measured[subset_slot] - forward
        current = current + back_project(residual, shifts, fraction, current.shape) / (NR * ANG)
        for tv_turn in range(TV_ITERS):
            current = tv_step(current)
    return current
```

```python
import functools

import jax
import jax.numpy as jnp
from jax import lax
from jax.experimental import pallas as pl
from jax.experimental.pallas import tpu as pltpu
from jax.sharding import PartitionSpec as P

SUBSETS = 2
NANG = 3000
TV_ITERS = 2
TV_STEP = 0.05
TV_EPS = 0.5
LANES = 128


class Sizes:
    def __init__(self, initial, measured, ray, cuts):
        self.slices, self.strip, self.breadth = initial.shape
        self.angles = measured.shape[1]
        self.ray, self.cuts = ray, cuts
        self.rows = self.strip * ray
        self.total_slices = self.slices * cuts
        self.half = (self.rows + 1) // 2
        self.taps = 2 * self.half + 1
        reach = SUBSETS * (2 * self.half + TV_ITERS)
        self.halo_tiles = -(-2 * reach // LANES)
        self.side = self.halo_tiles * (LANES // 2)
        self.cols = self.breadth // ray
        self.local = self.cols + self.halo_tiles * LANES
        self.image = self.slices * self.rows
        self.sino = self.angles * self.slices


def column_of(z, place, shape):
    lane = lax.broadcasted_iota(jnp.int32, shape, len(shape) - 1)
    return place * z.cols + jnp.where(lane < z.cols + z.side, lane, lane - z.local)


def window(z, ref, lead, target):
    base = target * z.cols
    parts = [ref[lead + (pl.ds(pl.multiple_of(base, LANES), z.cols),)]]
    last = z.breadth - LANES
    for j in range(z.halo_tiles):
        right = base + z.cols + j * LANES
        left = base + (j - z.halo_tiles) * LANES
        at_right = pl.multiple_of(jnp.minimum(right, last), LANES)
        at_left = pl.multiple_of(jnp.maximum(left, 0), LANES)
        tile_r = jnp.where(right <= last, ref[lead + (pl.ds(at_right, LANES),)], 0.0)
        tile_l = jnp.where(left >= 0, ref[lead + (pl.ds(at_left, LANES),)], 0.0)
        lane = j * LANES + lax.broadcasted_iota(jnp.int32, tile_r.shape, tile_r.ndim - 1)
        parts.append(jnp.where(lane < z.side, tile_r, tile_l))
    return jnp.concatenate(parts, axis=-1)


def pack_kernel(z, ref, *outs):
    place = lax.axis_index("ray")
    for step, out in enumerate(outs):
        target = lax.rem(place + step, z.ray)
        out[...] = window(z, ref, (slice(None),) * (len(ref.shape) - 1), target)


def split(value):
    high = value.astype(jnp.bfloat16)
    return high, (value - high.astype(jnp.float32)).astype(jnp.bfloat16)


def tap_weights(z, slope, row, offset):
    spread = slope * (row.astype(jnp.float32) - (z.rows - 1) / 2.0)
    floor_part = jnp.floor(spread)
    frac = spread - floor_part
    near = -floor_part.astype(jnp.int32)
    return jnp.where(offset == near, 1.0 - frac, 0.0) + jnp.where(offset == near - 1, frac, 0.0)


def project(z, x, slope_col):
    group = max(1, 256 // z.image)
    total = jnp.zeros((z.sino, z.local), jnp.float32)
    for first in range(0, z.taps, group):
        count = min(group, z.taps - first)
        shape = (z.sino, count * z.image)
        lane = lax.broadcasted_iota(jnp.int32, shape, 1)
        row = lax.rem(lane, z.rows)
        s_in = lax.rem(lane // z.rows, z.slices)
        offset = first - z.half + lane // z.image
        s_out = lax.rem(lax.broadcasted_iota(jnp.int32, shape, 0), z.slices)
        weight = jnp.where(s_in == s_out, tap_weights(z, slope_col, row, offset), 0.0)
        w_high, w_low = split(weight)
        rolled = [
            pltpu.roll(x, (z.half - first - k) % z.local, 1) if first + k != z.half else x
            for k in range(count)
        ]
        x_high, x_low = split(jnp.concatenate(rolled, axis=0))
        dot = functools.partial(jnp.dot, preferred_element_type=jnp.float32)
        total = total + (dot(w_high, x_high) + dot(w_high, x_low) + dot(w_low, x_high))
    return total


def back(z, residual, slope_row, taps_ref):
    r_high, r_low = split(residual)
    stacked = jnp.concatenate([r_high, r_low, r_high], axis=0)
    shape = (z.taps * z.image, 3 * z.sino)
    line = lax.broadcasted_iota(jnp.int32, shape, 0)
    row = lax.rem(line, z.rows)
    s_out = lax.rem(line // z.rows, z.slices)
    offset = line // z.image - z.half
    lane = lax.broadcasted_iota(jnp.int32, shape, 1)
    weight = jnp.where(
        lax.rem(lane, z.slices) == s_out, tap_weights(z, slope_row, row, offset), 0.0
    )
    w_high, w_low = split(weight)
    weights = jnp.where(lane < 2 * z.sino, w_high, w_low)
    taps_ref[...] = jnp.dot(weights, stacked, preferred_element_type=jnp.float32)
    total = taps_ref[z.half * z.image : (z.half + 1) * z.image, :]
    for k in range(z.taps):
        if k != z.half:
            term = taps_ref[k * z.image : (k + 1) * z.image, :]
            total = total + pltpu.roll(term, (k - z.half) % z.local, 1)
    return total


def tv_steps(z, slabs, place, first_slice):
    shape = slabs[0].shape
    column = column_of(z, place, shape)
    inside = (column >= 0) & (column < z.breadth)
    open_c = inside & (column < z.breadth - 1)
    open_r = lax.broadcasted_iota(jnp.int32, shape, 0) < z.rows - 1
    for _ in range(TV_ITERS):
        flows = []
        for k in range(len(slabs) - 1):
            here = slabs[k]
            ident = first_slice + k
            open_s = (ident >= 0) & (ident < z.total_slices - 1)
            step_s = jnp.where(open_s, slabs[k + 1] - here, 0.0)
            step_r = jnp.where(open_r, pltpu.roll(here, z.rows - 1, 0) - here, 0.0)
            step_c = jnp.where(open_c, pltpu.roll(here, z.local - 1, 1) - here, 0.0)
            scale = lax.rsqrt(
                step_s * step_s + step_r * step_r + step_c * step_c + TV_EPS * TV_EPS
            )
            flows.append((step_s * scale, step_r * scale, step_c * scale))
        done = []
        for k in range(1, len(slabs) - 1):
            flow_s, flow_r, flow_c = flows[k]
            spread = flow_s - flows[k - 1][0]
            spread = spread + flow_r - pltpu.roll(flow_r, 1, 0)
            spread = spread + flow_c - pltpu.roll(flow_c, 1, 1)
            done.append(jnp.where(inside, slabs[k] + TV_STEP * spread, 0.0))
        slabs = done
        first_slice = first_slice + 1
    return slabs


def first_forward_kernel(z, slope_col, *refs):
    pieces, (x_out, f_out, strips) = refs[: z.ray], refs[z.ray :]
    place = lax.axis_index("ray")
    for step, piece in enumerate(pieces):
        strips[lax.rem(place - step + z.ray, z.ray)] = piece[...]
    for s in range(z.slices):
        for r in range(z.ray):
            first = s * z.rows + r * z.strip
            x_out[first : first + z.strip, :] = strips[r, s]
    f_out[...] = project(z, x_out[...], slope_col[...])


def residual_back(z, slot, stored, forward, x, slope_row, scratch):
    taps_ref, kept, sem = scratch
    place = lax.axis_index("ray")
    distance = lax.rem(place - slot + z.ray, z.ray)
    for step, piece in enumerate(stored):

        @pl.when(distance == step)
        def _():
            copy = pltpu.make_async_copy(piece, kept, sem)
            copy.start()
            copy.wait()

    column = column_of(z, place, (z.sino, z.local))
    inside = (column >= 0) & (column < z.breadth)
    residual = jnp.where(inside, kept[...] - forward, 0.0)
    return x + back(z, residual, slope_row, taps_ref) * (1.0 / (z.rows * z.angles))


def first_back_kernel(z, slots, slope_row, x, f, *refs):
    stored, out, scratch = refs[: z.ray], refs[z.ray], refs[z.ray + 1 :]
    out[...] = residual_back(z, slots[0], stored, f[...], x[...], slope_row[...], scratch)


def read_slabs(z, own, low, high):
    blocks = []
    for ref in (low, own, high):
        blocks += [ref[s * z.rows : (s + 1) * z.rows, :] for s in range(ref.shape[0] // z.rows)]
    return blocks


def tv_all(z, own, low, high):
    first = lax.axis_index("cuts") * z.slices - TV_ITERS
    return tv_steps(z, read_slabs(z, own, low, high), lax.axis_index("ray"), first)


def middle_kernel(z, subset, slots, slope_col, slope_row, own, low, high, *refs):
    stored, out, scratch = refs[: z.ray], refs[z.ray], refs[z.ray + 1 :]
    x = jnp.concatenate(tv_all(z, own, low, high), axis=0)
    forward = project(z, x, slope_col[...])
    out[...] = residual_back(z, slots[subset], stored, forward, x, slope_row[...], scratch)


def last_kernel(z, own, low, high, *refs):
    outs, scratch = refs[: z.ray], refs[z.ray]
    for s, slab in enumerate(tv_all(z, own, low, high)):
        for r in range(z.ray):
            scratch[r, s] = slab[r * z.strip : (r + 1) * z.strip, : z.cols]
    place = lax.axis_index("ray")
    for step, out in enumerate(outs):
        out[...] = scratch[lax.rem(place + step, z.ray)]


def join_kernel(z, *refs):
    pieces, out = refs[: z.ray], refs[z.ray]
    place = lax.axis_index("ray")
    for step, piece in enumerate(pieces):
        source = lax.rem(place - step + z.ray, z.ray)
        out[:, :, pl.ds(pl.multiple_of(source * z.cols, LANES), z.cols)] = piece[...]


def call(kernel, name, outs, operands, kinds, scratch=()):
    space = {"v": pltpu.VMEM, "s": pltpu.SMEM, "a": pl.ANY}
    single = isinstance(outs[0], int)
    shapes = [outs] if single else list(outs)
    result = pl.pallas_call(
        kernel,
        name=name,
        out_shape=[jax.ShapeDtypeStruct(s, jnp.float32) for s in shapes],
        in_specs=[pl.BlockSpec(memory_space=space[k]) for k in kinds],
        out_specs=[pl.BlockSpec(memory_space=pltpu.VMEM) for _ in shapes],
        scratch_shapes=list(scratch),
    )(*operands)
    return result[0] if single else result


def spread_over_ray(z, pieces):
    got = [pieces[0]]
    for step in range(1, z.ray):
        pairs = [(i, (i + step) % z.ray) for i in range(z.ray)]
        got.append(lax.ppermute(pieces[step], "ray", pairs))
    return got


def neighbours(z, x):
    width = TV_ITERS * z.rows
    up = [(i, i + 1) for i in range(z.cuts - 1)]
    down = [(i + 1, i) for i in range(z.cuts - 1)]
    low = lax.ppermute(x[x.shape[0] - width :], "cuts", up)
    high = lax.ppermute(x[:width], "cuts", down)
    return low, high


def on_device(ray, cuts, initial, measured, order, angle_index):
    z = Sizes(initial, measured, ray, cuts)
    bind = lambda kernel, *more: functools.partial(kernel, z, *more)
    strips = call(
        bind(pack_kernel), "pack_x", [(z.slices, z.strip, z.local)] * ray, [initial], "v"
    )
    strips = spread_over_ray(z, strips)
    lines = measured.reshape(z.sino, z.breadth)
    stored = call(bind(pack_kernel), "pack_m", [(z.sino, z.local)] * ray, [lines], "v")
    stored = spread_over_ray(z, stored)

    slots = order[:SUBSETS]
    slopes = -1.0 + (2.0 * angle_index[slots].astype(jnp.float32) + 1.0) / NANG
    slopes = jnp.repeat(slopes, z.slices, axis=1)
    slope_col = slopes[:, :, None]
    slope_row = jnp.tile(slopes, (1, 3))[:, None, :]

    whole = (z.image, z.local)
    scratch = [
        pltpu.VMEM((z.taps * z.image, z.local), jnp.float32),
        pltpu.VMEM((z.sino, z.local), jnp.float32),
        pltpu.SemaphoreType.DMA,
    ]
    x, forward = call(
        bind(first_forward_kernel),
        "forward_0",
        [whole, (z.sino, z.local)],
        [slope_col[0], *strips],
        "v" * (1 + ray),
        [pltpu.VMEM((ray, z.slices, z.strip, z.local), jnp.float32)],
    )
    x = call(
        bind(first_back_kernel),
        "back_0",
        whole,
        [slots, slope_row[0], x, forward, *stored],
        "svvv" + "a" * ray,
        scratch,
    )
    for subset in range(1, SUBSETS):
        low, high = neighbours(z, x)
        x = call(
            bind(middle_kernel, subset),
            f"middle_{subset}",
            whole,
            [slots, slope_col[subset], slope_row[subset], x, low, high, *stored],
            "svvvvv" + "a" * ray,
            scratch,
        )
    low, high = neighbours(z, x)
    pieces = call(
        bind(last_kernel),
        "last",
        [(z.slices, z.strip, z.cols)] * ray,
        [x, low, high],
        "vvv",
        [pltpu.VMEM((ray, z.slices, z.strip, z.cols), jnp.float32)],
    )
    pieces = spread_over_ray(z, pieces)
    return call(
        bind(join_kernel), "join", (z.slices, z.strip, z.breadth), pieces, "v" * ray
    )


def solution(mesh):
    return jax.shard_map(
        functools.partial(on_device, mesh.shape["ray"], mesh.shape["cuts"]),
        mesh=mesh,
        in_specs=(P("cuts", "ray", None), P("ray", None, "cuts", None), P(), P()),
        out_specs=P("cuts", "ray", None),
        check_vma=False,
    )
```

```python
import functools

import jax
import jax.numpy as jnp
from jax import lax
from jax.experimental import pallas as pl
from jax.experimental.pallas import tpu as pltpu
from jax.sharding import PartitionSpec as P

SUBSETS = 2
NANG = 3000
TV_ITERS = 2
TV_STEP = 0.05
TV_EPS = 0.5
LANES = 128
SUBLANES = 8


class Sizes:
    def __init__(self, initial, measured, ray, cuts):
        self.slices, self.strip, self.breadth = initial.shape
        self.angles = measured.shape[1]
        self.ray, self.cuts = ray, cuts
        self.rows = self.strip * ray
        self.total_slices = self.slices * cuts
        self.half = (self.rows + 1) // 2
        self.taps = 2 * self.half + 1
        reach = SUBSETS * (2 * self.half + TV_ITERS)
        self.halo_tiles = -(-2 * reach // LANES)
        self.side = self.halo_tiles * (LANES // 2)
        self.cols = self.breadth // ray
        self.local = self.cols + self.halo_tiles * LANES
        self.image = self.slices * self.rows
        self.sino = self.angles * self.slices
        self.scale = 1.0 / (self.rows * self.angles)
        self.xor_ray = ray & (ray - 1) == 0
        self.paired = cuts % 2 == 0 and ray % 2 == 0
        self.keep = 8 * self.taps * self.image * self.local < 16 * 2**20

    def peer(self, place, step):
        return place ^ step if self.xor_ray else lax.rem(place + step, self.ray)

    def source(self, place, step):
        return place ^ step if self.xor_ray else lax.rem(place - step + self.ray, self.ray)

    def step_from(self, place, source):
        return place ^ source if self.xor_ray else lax.rem(place - source + self.ray, self.ray)


def iota(shape, dim):
    return lax.broadcasted_iota(jnp.int32, shape, dim)


def inside_image(z, shape):
    lane = iota(shape, len(shape) - 1)
    offset = jnp.where(lane < z.cols + z.side, lane, lane - z.local)
    column = lax.axis_index("ray") * z.cols + offset
    return column, (column >= 0) & (column < z.breadth)


def window(z, load, target):
    base = target * z.cols
    parts = [load(pl.multiple_of(base, LANES), z.cols)]
    last = z.breadth - LANES
    for j in range(z.halo_tiles):
        right = base + z.cols + j * LANES
        left = base + (j - z.halo_tiles) * LANES
        tile_r = load(pl.multiple_of(jnp.minimum(right, last), LANES), LANES)
        tile_l = load(pl.multiple_of(jnp.maximum(left, 0), LANES), LANES)
        tile_r = jnp.where(right <= last, tile_r, 0.0)
        tile_l = jnp.where(left >= 0, tile_l, 0.0)
        lane = j * LANES + iota(tile_r.shape, tile_r.ndim - 1)
        parts.append(jnp.where(lane < z.side, tile_r, tile_l))
    return jnp.concatenate(parts, axis=-1)


def split(value):
    high = value.astype(jnp.bfloat16)
    return high, (value - high.astype(jnp.float32)).astype(jnp.bfloat16)


def slopes_of(z, table, slot):
    index = table[...]
    kept = jnp.where(iota(index.shape, 0) == slot, index, 0)
    row = jnp.sum(kept, axis=0, keepdims=True).astype(jnp.float32)
    return -1.0 + (2.0 * row + 1.0) / NANG


def tent(distance):
    return jnp.maximum(1.0 - jnp.abs(distance), 0.0)


def centred(z, row):
    return row.astype(jnp.float32) - (z.rows - 1) / 2.0


def project(z, x, slopes, taps_ref):
    both = 2 * z.image
    x_high, x_low = split(x)
    stacked = jnp.concatenate([x_high, x_low], axis=0)
    for k in range(z.taps):
        shift = (z.half - k) % z.local
        rolled = pltpu.roll(stacked, shift, 1) if shift else stacked
        taps_ref[k * both : (k + 1) * both, :] = rolled
    square = (z.angles, z.angles)
    column = jnp.where(iota(square, 0) == iota(square, 1), slopes, 0.0)
    column = jnp.sum(column, axis=1, keepdims=True)
    column = jnp.concatenate([column] * z.slices, axis=0)
    group = max(1, LANES // both)
    shape = (z.sino, group * both)
    line, lane = iota(shape, 0), iota(shape, 1)
    same = line // z.angles == lax.rem(lane // z.rows, z.slices)
    distance = column * centred(z, lax.rem(lane, z.rows)) + (lane // both).astype(jnp.float32)
    distance = jnp.where(same, distance, 4.0 * z.rows)
    on_high = lax.rem(lane // z.image, 2) == 0
    highs, lows = [], []
    for first in range(0, z.taps, group):
        w_high, w_low = split(tent(distance + float(first - z.half)))
        w_low = jnp.where(on_high, w_low, jnp.zeros_like(w_low))
        keep = min(group, z.taps - first) * both
        highs.append(w_high[:, :keep])
        lows.append(w_low[:, :keep])
    weights = jnp.concatenate(
        [jnp.concatenate(highs, axis=1), jnp.concatenate(lows, axis=1)], axis=0
    )
    result = jnp.dot(weights, taps_ref[...], preferred_element_type=jnp.float32)
    return result[: z.sino] + result[z.sino :]


def back_weights(z, slopes):
    row = jnp.concatenate([slopes] * (2 * z.slices), axis=1)
    shape = (z.image, 2 * z.sino)
    line, lane = iota(shape, 0), iota(shape, 1)
    same = line // z.rows == lax.rem(lane // z.angles, z.slices)
    distance = jnp.where(same, row * centred(z, lax.rem(line, z.rows)), 4.0 * z.rows)
    parts = []
    for k in range(z.taps):
        w_high, w_low = split(tent(distance + float(k - z.half)))
        parts.append(jnp.concatenate([w_high, w_low[:, : z.sino]], axis=1))
    return jnp.concatenate(parts, axis=0)


def back(z, residual, weights, taps_ref):
    r_high, r_low = split(residual)
    stacked = jnp.concatenate([r_high, r_low, r_high], axis=0)
    taps_ref[...] = jnp.dot(weights, stacked, preferred_element_type=jnp.float32)
    tiles = []
    for first in range(0, z.image, SUBLANES):
        total = None
        for k in range(z.taps):
            at = k * z.image + first
            term = taps_ref[at : at + SUBLANES, :]
            shift = (k - z.half) % z.local
            term = pltpu.roll(term, shift, 1) if shift else term
            total = term if total is None else total + term
        tiles.append(total)
    return jnp.concatenate(tiles, axis=0)


def tv_steps(z, slabs):
    shape = slabs[0].shape
    column, inside = inside_image(z, shape)
    open_c = inside & (column < z.breadth - 1)
    open_r = iota(shape, 0) < z.rows - 1
    first_own = lax.axis_index("cuts") == 0
    last_own = lax.axis_index("cuts") == z.cuts - 1
    for turn in range(TV_ITERS):
        before = TV_ITERS - 1 - turn
        flows = []
        for k in range(len(slabs) - 1):
            here = slabs[k]
            step_s = slabs[k + 1] - here
            if k == before:
                step_s = jnp.where(first_own, 0.0, step_s)
            if k == before + z.slices:
                step_s = jnp.where(last_own, 0.0, step_s)
            step_r = jnp.where(open_r, pltpu.roll(here, z.rows - 1, 0) - here, 0.0)
            step_c = jnp.where(open_c, pltpu.roll(here, z.local - 1, 1) - here, 0.0)
            scale = lax.rsqrt(
                step_s * step_s + step_r * step_r + step_c * step_c + TV_EPS * TV_EPS
            )
            flows.append((step_s * scale, step_r * scale, step_c * scale))
        done = []
        for k in range(1, len(slabs) - 1):
            flow_s, flow_r, flow_c = flows[k]
            spread = flow_s - flows[k - 1][0]
            spread = spread + flow_r - pltpu.roll(flow_r, 1, 0)
            spread = spread + flow_c - pltpu.roll(flow_c, 1, 1)
            done.append(slabs[k] + TV_STEP * spread)
        slabs = done
    return [jnp.where(inside, slab, 0.0) for slab in slabs]


def tv_all(z, own, first, second):
    def slab(ref, s):
        return ref[s * z.rows : (s + 1) * z.rows, :]

    odd = lax.rem(lax.axis_index("cuts"), 2) == 1

    def side(one, two, s):
        if not z.paired:
            return slab(one, s)
        return jnp.where(odd, slab(one, s), slab(two, s))

    low = [side(first, second, s) for s in range(z.slices - TV_ITERS, z.slices)]
    high = [side(second, first, s) for s in range(TV_ITERS)]
    return tv_steps(z, low + [slab(own, s) for s in range(z.slices)] + high)


def measured_back(z, steps, measured, table, outs, taps_ref):
    place = lax.axis_index("ray")
    weights = back_weights(z, slopes_of(z, table, place))
    for step, out in zip(steps, outs):
        target = z.peer(place, step)
        lines = [
            window(z, lambda at, size, s=s: measured[0, :, s, pl.ds(at, size)], target)
            for s in range(z.slices)
        ]
        out[...] = back(z, jnp.concatenate(lines, axis=0), weights, taps_ref)


def start_kernel(z, steps, initial, measured, table, *refs):
    strips, outs, taps_ref = refs[: z.ray], refs[z.ray : -1], refs[-1]
    place = lax.axis_index("ray")
    for step, out in enumerate(strips):
        out[...] = window(
            z, lambda at, size: initial[:, :, pl.ds(at, size)], z.peer(place, step)
        )
    measured_back(z, steps, measured, table, outs, taps_ref)


def more_kernel(z, steps, measured, table, *refs):
    measured_back(z, steps, measured, table, refs[:-1], refs[-1])


def modelled_update(z, slot, table, x, x_taps, r_taps):
    slopes = slopes_of(z, table, slot)
    forward = project(z, x, slopes, x_taps)
    _, inside = inside_image(z, forward.shape)
    forward = jnp.where(inside, forward, 0.0)
    return x - back(z, forward, back_weights(z, slopes), r_taps) * z.scale


def add_measured(z, slot, stored, value, out):
    wanted = z.step_from(lax.axis_index("ray"), slot)
    for step, piece in enumerate(stored):

        @pl.when(wanted == step)
        def _():
            out[...] = value + piece[...] * z.scale


def first_kernel(z, order, table, *refs):
    pieces, (out, strips, x_taps, r_taps) = refs[: z.ray], refs[z.ray :]
    place = lax.axis_index("ray")
    for step, piece in enumerate(pieces):
        strips[z.source(place, step)] = piece[...]
    x = jnp.concatenate(
        [strips[r, s] for s in range(z.slices) for r in range(z.ray)], axis=0
    )
    out[...] = modelled_update(z, order[0], table, x, x_taps, r_taps)


def add_kernel(z, order, value, *refs):
    add_measured(z, order[0], refs[: z.ray], value[...], refs[z.ray])


def middle_kernel(z, subset, order, table, own, first, second, *refs):
    stored, (out, x_taps, r_taps) = refs[: z.ray], refs[z.ray :]
    x = jnp.concatenate(tv_all(z, own, first, second), axis=0)
    value = modelled_update(z, order[subset], table, x, x_taps, r_taps)
    add_measured(z, order[subset], stored, value, out)


def last_kernel(z, own, first, second, *refs):
    outs, rows = refs[: z.ray], refs[z.ray]
    for s, slab in enumerate(tv_all(z, own, first, second)):
        for r in range(z.ray):
            rows[r, s] = slab[r * z.strip : (r + 1) * z.strip, : z.cols]
    place = lax.axis_index("ray")
    for step, out in enumerate(outs):
        out[...] = rows[z.peer(place, step)]


def join_kernel(z, *refs):
    pieces, out = refs[: z.ray], refs[z.ray]
    place = lax.axis_index("ray")
    for step, piece in enumerate(pieces):
        at = pl.multiple_of(z.source(place, step) * z.cols, LANES)
        out[:, :, pl.ds(at, z.cols)] = piece[...]


def call(kernel, name, outs, operands, kinds, scratch=(), keep=True):
    keep = keep and kernel.args[0].keep
    single = isinstance(outs[0], int)
    shapes = [outs] if single else list(outs)
    make = pltpu.VMEM if keep else jax.ShapeDtypeStruct
    operands = [
        pltpu.with_memory_space_constraint(value, pltpu.VMEM)
        if kind == "v" and kernel.args[0].keep
        else value
        for value, kind in zip(operands, kinds)
    ]
    result = pl.pallas_call(
        kernel,
        name=name,
        out_shape=[make(shape, jnp.float32) for shape in shapes],
        in_specs=[
            pl.BlockSpec(memory_space=pltpu.SMEM if kind == "s" else pltpu.VMEM)
            for kind in kinds
        ],
        out_specs=[pl.BlockSpec(memory_space=pltpu.VMEM) for _ in shapes],
        scratch_shapes=list(scratch),
    )(*operands)
    return result[0] if single else result


def swap_over_ray(z, pieces, steps):
    got = []
    for step, piece in zip(steps, pieces):
        if step == 0:
            got.append(piece)
            continue
        if z.xor_ray:
            pairs = [(i, i ^ step) for i in range(z.ray)]
        else:
            pairs = [(i, (i + step) % z.ray) for i in range(z.ray)]
        got.append(lax.ppermute(piece, "ray", pairs))
    return got


def neighbours(z, x):
    if not z.paired:
        up = [(i, i + 1) for i in range(z.cuts - 1)]
        down = [(i + 1, i) for i in range(z.cuts - 1)]
        return lax.ppermute(x, "cuts", up), lax.ppermute(x, "cuts", down)
    even = [(c, c ^ 1) for c in range(z.cuts)]
    odd = []
    for r in range(z.ray):
        for c in range(z.cuts):
            if c in (0, z.cuts - 1):
                to = (r ^ 1) * z.cuts + c
            else:
                to = r * z.cuts + (c + 1 if c % 2 else c - 1)
            odd.append((r * z.cuts + c, to))
    return lax.ppermute(x, "cuts", even), lax.ppermute(x, ("ray", "cuts"), odd)


def on_device(ray, cuts, initial, measured, order, angle_index):
    z = Sizes(initial, measured, ray, cuts)
    bind = lambda kernel, *more: functools.partial(kernel, z, *more)
    whole = (z.image, z.local)
    x_taps = pltpu.VMEM((2 * z.taps * z.image, z.local), jnp.bfloat16)
    r_taps = pltpu.VMEM((z.taps * z.image, z.local), jnp.float32)

    steps = list(range(2, ray)) + list(range(min(2, ray)))
    head, tail = steps[:2], steps[2:]
    outs = call(
        bind(start_kernel, head),
        "start",
        [(z.slices, z.strip, z.local)] * ray + [whole] * len(head),
        [initial, measured, angle_index],
        "ppp",
        [r_taps],
    )
    strips = swap_over_ray(z, outs[:ray], range(ray))
    stored = dict(zip(head, swap_over_ray(z, outs[ray:], head)))
    while tail:
        head, tail = tail[:2], tail[2:]
        outs = call(
            bind(more_kernel, head),
            "more",
            [whole] * len(head),
            [measured, angle_index],
            "pp",
            [r_taps],
        )
        stored.update(zip(head, swap_over_ray(z, outs, head)))
    stored = [stored[step] for step in range(ray)]

    value = call(
        bind(first_kernel),
        "first",
        whole,
        [order, angle_index, *strips],
        "sp" + "v" * ray,
        [pltpu.VMEM((ray, z.slices, z.strip, z.local), jnp.float32), x_taps, r_taps],
    )
    x = call(bind(add_kernel), "add", whole, [order, value, *stored], "sv" + "v" * ray)
    for subset in range(1, SUBSETS):
        x = call(
            bind(middle_kernel, subset),
            f"middle_{subset}",
            whole,
            [order, angle_index, x, *neighbours(z, x), *stored],
            "spvvv" + "v" * ray,
            [x_taps, r_taps],
        )
    pieces = call(
        bind(last_kernel),
        "last",
        [(z.slices, z.strip, z.cols)] * ray,
        [x, *neighbours(z, x)],
        "vvv",
        [pltpu.VMEM((ray, z.slices, z.strip, z.cols), jnp.float32)],
    )
    return call(
        bind(join_kernel),
        "join",
        (z.slices, z.strip, z.breadth),
        swap_over_ray(z, pieces, range(ray)),
        "v" * ray,
        keep=False,
    )


def solution(mesh):
    return jax.shard_map(
        functools.partial(on_device, mesh.shape["ray"], mesh.shape["cuts"]),
        mesh=mesh,
        in_specs=(P("cuts", "ray", None), P("ray", None, "cuts", None), P(), P()),
        out_specs=P("cuts", "ray", None),
        check_vma=False,
    )
```
